128 devices in a mesh: dp: 4 (over y_hi, core), feat: 32 (over y_lo, x, z).
Axes of the slice: x: 4, y: 4 (y_hi: 2, y_lo: 2; y = y_hi * 2 + y_lo), z: 4, core: 2. Of those that a mesh axis runs over, the one named last changes fastest.
Arguments:
- tokens: bfloat16 [4096, 65536], P('dp', 'feat'), may hold values from -6 to 6
- left_factor: bfloat16 [256, 256, 256], P('feat'), may hold values from -0.375 to 0.375
- right_factor: bfloat16 [256, 256, 256], P('feat'), may hold values from -0.375 to 0.375
- cotangent: bfloat16 [4096, 65536], P('dp', 'feat'), may hold values from -6 to 6
Outputs:
- output: bfloat16 [4096, 65536], P('dp', 'feat')
- input_grad: bfloat16 [4096, 65536], P('dp', 'feat')
- left_grad: float32 [256, 256, 256], P('feat')
- right_grad: float32 [256, 256, 256], P('feat')
The draws below stay inside these ranges and needn't reach their ends.
All inputs are finite; a program needn't handle non-finite values.
Results may differ from the reference program's by a relative error of at most 0.0058.
Values may be sent and summed in bfloat16 or wider, within the bound.
A program may use at most 128 MiB of HBM per device.

```python
import math
import jax
import jax.numpy as jnp
from jax import lax

BLOCKS = 256
BLOCK = 256
TOK_DEV = 1024
WIDTH = 65536
TOKENS = 4096
N_DP = 4


def levels(rng, dims, split, least, top_value):
    def one(position, shards_of):
        steps = jax.random.uniform(jax.random.fold_in(jax.random.fold_in(rng, 6), position), (shards_of,), jnp.float32, least / len(split), top_value / len(split))
        return jnp.repeat(jnp.exp(steps), dims[position] // shards_of).reshape((-1,) + (1,) * (len(dims) - position - 1))

    loudness = one(*split[0])
    for cut in split[1:]:
        loudness = loudness * one(*cut)
    return loudness


def centred(rng, shape, scale, limit, cuts=(), dtype=jnp.bfloat16):
    drawn = jax.random.normal(rng, shape, jnp.float32) * scale
    if len(cuts) > 0:
        drawn = levels(rng, shape, cuts, -0.22, 0.18) * drawn
    return jnp.clip(drawn, min=-limit, max=limit).astype(dtype)


def setup_inputs(seed: int = 0) -> dict:
    arg_keys = jax.random.split(jax.random.key(seed), 5)
    return {
        "tokens": centred(arg_keys[0], (TOKENS, WIDTH), 1.0, 6.0, ((0, 4), (1, 32))),
        "left_factor": centred(arg_keys[1], (BLOCKS, BLOCK, BLOCK), BLOCK ** -0.5, 0.375, ((0, 32),)),
        "right_factor": centred(arg_keys[2], (BLOCK, BLOCKS, BLOCKS), BLOCKS ** -0.5, 0.375, ((0, 32),)),
        "cotangent": centred(arg_keys[3], (TOKENS, WIDTH), 1.0, 6.0, ((0, 4), (1, 32))),
    }


SQRT_HALF = 0.7071067811865476
INV_ROOT_TWO_PI = 0.3989422804014327

def gelu_exact(value):
    return 0.5 * value * (1.0 + jax.scipy.special.erf(value * SQRT_HALF))

def gelu_slope(value):
    cumulative = 0.5 * (1.0 + jax.scipy.special.erf(value * SQRT_HALF))
    return cumulative + value * jnp.exp(-0.5 * value * value) * INV_ROOT_TWO_PI

def reference(tokens, left_factor, right_factor, cotangent):
    inputs_all = tokens.reshape(N_DP, TOK_DEV, BLOCKS, BLOCK)
    upstream_all = cotangent.reshape(N_DP, TOK_DEV, BLOCK, BLOCKS)
    left_wide = left_factor.astype(jnp.float32)
    right_wide = right_factor.astype(jnp.float32)

    def accumulate(totals, pieces):
        blocked, upstream = pieces
        blocked_wide = blocked.astype(jnp.float32)
        upstream_wide = upstream.astype(jnp.float32)
        preact = jnp.einsum('tba,baj->tbj', blocked_wide, left_wide)
        activated = gelu_exact(preact).astype(jnp.bfloat16)
        activated_wide = activated.astype(jnp.float32)
        mixed = jnp.einsum('tbj,jbk->tjk', activated_wide, right_wide).astype(jnp.bfloat16)
        returned = jnp.einsum('tjk,jbk->tbj', upstream_wide, right_wide).astype(jnp.bfloat16)
        preact_grad = (returned.astype(jnp.float32) * gelu_slope(preact)).astype(jnp.bfloat16)
        grad_wide = preact_grad.astype(jnp.float32)
        input_grad = jnp.einsum('tbj,baj->tba', grad_wide, left_wide).astype(jnp.bfloat16)
        left_total = totals[0] + jnp.einsum('tba,tbj->baj', blocked_wide, grad_wide)
        right_total = totals[1] + jnp.einsum('tbj,tjk->jbk', activated_wide, upstream_wide)
        return ((left_total, right_total), (mixed.reshape(TOK_DEV, BLOCKS * BLOCK), input_grad.reshape(TOK_DEV, BLOCKS * BLOCK)))
    start = (jnp.zeros((BLOCKS, BLOCK, BLOCK), jnp.float32), jnp.zeros((BLOCK, BLOCKS, BLOCKS), jnp.float32))
    totals, results = lax.scan(accumulate, start, (inputs_all, upstream_all))
    norm_factor = 1.0 / math.sqrt(TOKENS)
    output = results[0].reshape(TOKENS, BLOCKS * BLOCK)
    input_grad = results[1].reshape(TOKENS, BLOCKS * BLOCK)
    return (output, input_grad, totals[0] * norm_factor, totals[1] * norm_factor)
```

```python
import math

import jax
import jax.numpy as jnp
from jax import lax
from jax.experimental import pallas as pl
from jax.experimental.pallas import tpu as pltpu
from jax.sharding import PartitionSpec as P

SQRT_HALF = 0.7071067811865476
INV_ROOT_TWO_PI = 0.3989422804014327
MESH = pl.DeviceIdType.MESH
F32 = jnp.float32
BF16 = jnp.bfloat16
NT = (((1,), (1,)), ((), ()))
TN = (((0,), (0,)), ((), ()))
TT = (((0,), (1,)), ((), ()))
NF = 32
NB = 8
T = 1024
W = 256
H = 128
ORDER = [(13 * k) % NF for k in range(1, NF)]


def dot(a, b, dims=(((1,), (0,)), ((), ()))):
    return lax.dot_general(a, b, dims, preferred_element_type=F32)


def kernel(
    tok, lf, rf, ct, out, ig, lg, rg,
    x_v, c_v, l_v, r_v, send_d, recv_d, pre_v, send_a, recv_a, out_v, ig_v,
    keep_v, s1_v, r1_v, s2_v, r2_v, grad_v,
    x_sem, c_sem, w_sem, sd_sem, rd_sem, sa_sem, ra_sem, out_sem, ig_sem,
    s1_sem, r1_sem, s2_sem, r2_sem, s3_sem, r3_sem, g_sem,
):
    dp = lax.axis_index("dp")
    me = lax.axis_index("feat")
    core = dp % 2
    sibling = (dp + 1 - 2 * core, me)
    across = ((dp + 2) % 4, me)
    my, mx, mz = me // 16, (me // 4) % 4, me % 4
    peers = [
        ((my + p // 16) % 2) * 16 + ((mx + (p // 4) % 4) % 4) * 4 + (mz + p % 4) % 4 for p in ORDER
    ]

    def cols(n):
        return pl.ds(pl.multiple_of(n * W, W), W)

    pltpu.make_async_copy(rf, r_v, w_sem.at[0]).start()

    @pl.loop(0, NB)
    def _(n):
        pltpu.make_async_copy(ct.at[:, cols(n)], c_v.at[n], c_sem.at[n]).start()

    pltpu.make_async_copy(lf, l_v, w_sem.at[1]).start()

    @pl.loop(0, NB)
    def _(n):
        pltpu.make_async_copy(tok.at[:, cols(n)], x_v.at[n], x_sem.at[n]).start()

    barrier = pltpu.get_barrier_semaphore()
    for p in peers:
        pl.semaphore_signal(barrier, inc=1, device_id=(dp, p), device_id_type=MESH)
    for d in (sibling, across):
        pl.semaphore_signal(barrier, inc=1, device_id=d, device_id_type=MESH)

    def compute_d(i):
        pltpu.make_async_copy(ct.at[:, cols(i)], c_v.at[i], c_sem.at[i]).wait()
        v = dot(r_v[i], c_v[i], NT)
        send_d[i] = v.reshape(NF, NB, T).astype(BF16)

    pltpu.make_async_copy(rf, r_v, w_sem.at[0]).wait()
    compute_d(0)
    pl.semaphore_wait(barrier, NF + 1)

    @pl.loop(0, NB)
    def _(i):
        for p in peers:
            pltpu.make_async_remote_copy(
                src_ref=send_d.at[i, p], dst_ref=recv_d.at[me * NB + i],
                send_sem=sd_sem.at[i], recv_sem=rd_sem.at[i],
                device_id=(dp, p), device_id_type=MESH,
            ).start()
        pltpu.make_async_copy(send_d.at[i, me], recv_d.at[me * NB + i], rd_sem.at[i]).start()

        @pl.when(i < NB - 1)
        def _():
            compute_d(i + 1)

    pltpu.make_async_copy(lf, l_v, w_sem.at[1]).wait()

    @pl.loop(0, NB)
    def _(b):
        pltpu.make_async_copy(tok.at[:, cols(b)], x_v.at[b], x_sem.at[b]).wait()
        v = dot(l_v[b], x_v[b], TT)
        for q in range(T // H):
            pre_v[q, pl.ds(b, W, stride=NB), :] = v[:, q * H:(q + 1) * H]

    @pl.loop(0, NB)
    def _(i):
        @pl.loop(0, NF)
        def _(d):
            j = d * NB + i
            rows = pl.ds(pl.multiple_of(j * NB, NB), NB)
            for q in range(T // H):
                u = pre_v[q, rows, :]
                half = 0.5 * (1.0 + lax.erf(u * SQRT_HALF))
                send_a[j, :, q * H:(q + 1) * H] = (u * half).astype(BF16)
                pre_v[q, rows, :] = half + u * jnp.exp(-0.5 * u * u) * INV_ROOT_TWO_PI

        for p in peers:
            pltpu.make_async_remote_copy(
                src_ref=send_a.at[p * NB + i], dst_ref=recv_a.at[i, me],
                send_sem=sa_sem.at[i], recv_sem=ra_sem.at[i],
                device_id=(dp, p), device_id_type=MESH,
            ).start()
        pltpu.make_async_copy(send_a.at[me * NB + i], recv_a.at[i, me], ra_sem.at[i]).start()

    mine = pl.ds(pl.multiple_of(core * H, H), H)
    other = pl.ds(pl.multiple_of((1 - core) * H, H), H)

    def hop1(g):
        return pltpu.make_async_remote_copy(
            src_ref=s1_v.at[g], dst_ref=r1_v.at[g], send_sem=s1_sem.at[g], recv_sem=r1_sem.at[g],
            device_id=sibling, device_id_type=MESH)

    def hop2(g):
        return pltpu.make_async_remote_copy(
            src_ref=s2_v.at[g], dst_ref=r2_v.at[g], send_sem=s2_sem.at[g], recv_sem=r2_sem.at[g],
            device_id=across, device_id_type=MESH)

    def hop3(g):
        return pltpu.make_async_remote_copy(
            src_ref=grad_v.at[g, mine], dst_ref=grad_v.at[g, mine], send_sem=s3_sem.at[g], recv_sem=r3_sem.at[g],
            device_id=sibling, device_id_type=MESH)

    def first(g, value):
        keep_v[...] = value
        r2_own = keep_v[mine, :]
        s1_v[g] = keep_v[other, :]
        hop1(g).start()
        grad_v[g, mine] = r2_own

    def second(g):
        hop1(g).wait_recv()
        s2_v[g] = (grad_v[g, mine] + r1_v[g]).astype(BF16)
        hop2(g).start()

    norm = 1.0 / math.sqrt(T * 4)

    def third(g):
        hop2(g).wait_recv()
        grad_v[g, mine] = (s2_v[g].astype(F32) + r2_v[g].astype(F32)) * norm
        hop3(g).start()

    @pl.loop(0, NB)
    def _(i):
        pltpu.make_async_copy(send_d.at[i], send_d.at[i], rd_sem.at[i]).wait()

    @pl.loop(0, NF * NB)
    def _(j):
        rows = pl.ds(pl.multiple_of(j * NB, NB), NB)
        for q in range(T // H):
            pre_v[q, rows, :] = pre_v[q, rows, :] * recv_d[j, :, q * H:(q + 1) * H].astype(F32)

    def put_ig(b):
        return pltpu.make_async_copy(ig_v.at[b % 2], ig.at[:, cols(b)], ig_sem.at[b % 2])

    @pl.loop(0, NB)
    def _(b):
        g = jnp.concatenate(
            [pre_v[q, pl.ds(b, W, stride=NB), :].astype(BF16) for q in range(T // H)], axis=1)

        @pl.when(b >= 2)
        def _():
            put_ig(b - 2).wait()

        ig_v[b % 2] = dot(g, l_v[b], TT).astype(BF16)
        put_ig(b).start()
        first(b, dot(g, x_v[b]).T)

        @pl.when(b >= 1)
        def _():
            second(b - 1)

    for b in range(NB - 2, NB):
        put_ig(b).wait()

    def put_out(i):
        return pltpu.make_async_copy(out_v.at[i % 2], out.at[:, cols(i)], out_sem.at[i % 2])

    @pl.loop(0, NB)
    def _(i):
        pltpu.make_async_copy(send_d.at[i], send_d.at[i], ra_sem.at[i]).wait()
        a = recv_a[i].astype(F32).reshape(W, T).astype(BF16)
        first(NB + i, dot(a, c_v[i]))

        @pl.when(i >= 2)
        def _():
            put_out(i - 2).wait()

        out_v[i % 2] = dot(a, r_v[i], TN).astype(BF16)
        put_out(i).start()
        second(NB + i - 1)
        third(i)

        @pl.when(i >= 2)
        def _():
            third(NB + i - 2)

    second(2 * NB - 1)
    third(2 * NB - 2)
    third(2 * NB - 1)

    for b in range(NB - 2, NB):
        put_out(b).wait()

    @pl.loop(0, 2 * NB)
    def _(g):
        hop3(g).wait_recv()
        hop1(g).wait_send()
        hop2(g).wait_send()
        hop3(g).wait_send()

    @pl.loop(0, NB)
    def _(i):
        pltpu.make_async_remote_copy(
            src_ref=send_d.at[i, pl.ds(0, NF - 1)], dst_ref=recv_d.at[pl.ds(0, NF - 1)],
            send_sem=sd_sem.at[i], recv_sem=rd_sem.at[i], device_id=sibling, device_id_type=MESH).wait_send()
        pltpu.make_async_remote_copy(
            src_ref=send_d.at[i, pl.ds(0, NF - 1)], dst_ref=recv_d.at[pl.ds(0, NF - 1)],
            send_sem=sa_sem.at[i], recv_sem=ra_sem.at[i], device_id=sibling, device_id_type=MESH).wait_send()

    a = pltpu.make_async_copy(grad_v.at[pl.ds(0, NB)], lg, g_sem.at[0])
    b = pltpu.make_async_copy(grad_v.at[pl.ds(NB, NB)], rg, g_sem.at[1])
    a.start()
    b.start()
    a.wait()
    b.wait()


def local(tokens, left_factor, right_factor, cotangent):
    any_spec = pl.BlockSpec(memory_space=pl.ANY)
    dma = pltpu.SemaphoreType.DMA
    return pl.pallas_call(
        kernel,
        out_shape=(
            jax.ShapeDtypeStruct(tokens.shape, BF16),
            jax.ShapeDtypeStruct(tokens.shape, BF16),
            jax.ShapeDtypeStruct(left_factor.shape, F32),
            jax.ShapeDtypeStruct(right_factor.shape, F32),
        ),
        in_specs=[any_spec] * 4,
        out_specs=(any_spec,) * 4,
        scratch_shapes=[
            pltpu.VMEM((NB, T, W), BF16), pltpu.VMEM((NB, T, W), BF16),
            pltpu.VMEM((NB, W, W), BF16), pltpu.VMEM((NB, W, W), BF16),
            pltpu.VMEM((NB, NF, NB, T), BF16), pltpu.VMEM((NF * NB, NB, T), BF16),
            pltpu.VMEM((T // H, W * NB, H), F32),
            pltpu.VMEM((NF * NB, NB, T), BF16), pltpu.VMEM((NB, NF, NB, T), BF16),
            pltpu.VMEM((2, T, W), BF16), pltpu.VMEM((2, T, W), BF16),
            pltpu.VMEM((W, W), F32),
            pltpu.VMEM((2 * NB, H, W), F32), pltpu.VMEM((2 * NB, H, W), F32),
            pltpu.VMEM((2 * NB, H, W), BF16), pltpu.VMEM((2 * NB, H, W), BF16),
            pltpu.VMEM((2 * NB, W, W), F32),
            dma((NB,)), dma((NB,)), dma((2,)), dma((NB,)), dma((NB,)), dma((NB,)), dma((NB,)), dma((2,)), dma((2,)),
            dma((2 * NB,)), dma((2 * NB,)), dma((2 * NB,)), dma((2 * NB,)), dma((2 * NB,)), dma((2 * NB,)), dma((2,)),
        ],
        compiler_params=pltpu.CompilerParams(
            collective_id=0, has_side_effects=True, vmem_limit_bytes=63 << 20),
        name="monarch",
    )(tokens, left_factor, right_factor, cotangent)


def solution(mesh):
    in_specs = (P("dp", "feat"), P("feat", None, None), P("feat", None, None), P("dp", "feat"))
    out_specs = (P("dp", "feat"), P("dp", "feat"), P("feat", None, None), P("feat", None, None))
    return jax.shard_map(local, mesh=mesh, in_specs=in_specs, out_specs=out_specs, check_vma=False)
```

```python
import math

import jax
import jax.numpy as jnp
from jax import lax
from jax.experimental import pallas as pl
from jax.experimental.pallas import tpu as pltpu
from jax.sharding import PartitionSpec as P

SQRT_HALF = 0.7071067811865476
INV_ROOT_TWO_PI = 0.3989422804014327
MESH = pl.DeviceIdType.MESH
F32 = jnp.float32
BF16 = jnp.bfloat16
NT = (((1,), (1,)), ((), ()))
TN = (((0,), (0,)), ((), ()))
TT = (((0,), (1,)), ((), ()))
NF = 32
NB = 8
T = 1024
W = 256
H = 128
ORDER = sorted([(13 * k) % NF for k in range(1, NF)], key=lambda p: p < NF // 2)


def dot(a, b, dims=(((1,), (0,)), ((), ()))):
    return lax.dot_general(a, b, dims, preferred_element_type=F32)


def kernel(
    tok, lf, rf, ct, c_v, x_v, grad_v,
    l_v, r_v, send_d, recv_d, pre_v, send_a, recv_a,
    keep_v, s1_v, r1_v, s2_v, r2_v,
    x_sem, c_sem, w_sem, sd_sem, rd_sem, sa_sem, ra_sem,
    s1_sem, r1_sem, s2_sem, r2_sem, s3_sem, r3_sem,
):
    dp = lax.axis_index("dp")
    me = lax.axis_index("feat")
    core = dp % 2
    sibling = (dp + 1 - 2 * core, me)
    across = ((dp + 2) % 4, me)
    my, mx, mz = me // 16, (me // 4) % 4, me % 4
    peers = [
        ((my + p // 16) % 2) * 16 + ((mx + (p // 4) % 4) % 4) * 4 + (mz + p % 4) % 4 for p in ORDER
    ]

    def cols(n):
        return pl.ds(pl.multiple_of(n * W, W), W)

    pltpu.make_async_copy(rf, r_v, w_sem.at[0]).start()

    @pl.loop(0, NB)
    def _(n):
        pltpu.make_async_copy(ct.at[:, cols(n)], c_v.at[n], c_sem.at[n]).start()

    pltpu.make_async_copy(lf, l_v, w_sem.at[1]).start()

    @pl.loop(0, NB)
    def _(n):
        pltpu.make_async_copy(tok.at[:, cols(n)], x_v.at[n], x_sem.at[n]).start()

    barrier = pltpu.get_barrier_semaphore()
    for p in peers:
        pl.semaphore_signal(barrier, inc=1, device_id=(dp, p), device_id_type=MESH)
    for d in (sibling, across):
        pl.semaphore_signal(barrier, inc=1, device_id=d, device_id_type=MESH)

    def compute_d(i):
        pltpu.make_async_copy(ct.at[:, cols(i)], c_v.at[i], c_sem.at[i]).wait()
        v = dot(r_v[i], c_v[i], NT)
        send_d[i] = v.reshape(NF, NB, T).astype(BF16)

    pltpu.make_async_copy(rf, r_v, w_sem.at[0]).wait()
    compute_d(0)
    pl.semaphore_wait(barrier, NF + 1)

    @pl.loop(0, NB)
    def _(i):
        for p in peers:
            pltpu.make_async_remote_copy(
                src_ref=send_d.at[i, p], dst_ref=recv_d.at[me * NB + i],
                send_sem=sd_sem.at[i], recv_sem=rd_sem.at[i],
                device_id=(dp, p), device_id_type=MESH,
            ).start()
        pltpu.make_async_copy(send_d.at[i, me], recv_d.at[me * NB + i], rd_sem.at[i]).start()

        @pl.when(i < NB - 1)
        def _():
            compute_d(i + 1)

    pltpu.make_async_copy(lf, l_v, w_sem.at[1]).wait()

    @pl.loop(0, NB)
    def _(b):
        pltpu.make_async_copy(tok.at[:, cols(b)], x_v.at[b], x_sem.at[b]).wait()
        v = dot(l_v[b], x_v[b], TT)
        for q in range(T // H):
            pre_v[q, pl.ds(b, W, stride=NB), :] = v[:, q * H:(q + 1) * H]

    def push_a(i):
        for p in peers:
            pltpu.make_async_remote_copy(
                src_ref=send_a.at[p * NB + i], dst_ref=recv_a.at[i, me],
                send_sem=sa_sem.at[i], recv_sem=ra_sem.at[i],
                device_id=(dp, p), device_id_type=MESH,
            ).start()
        pltpu.make_async_copy(send_a.at[me * NB + i], recv_a.at[i, me], ra_sem.at[i]).start()

    @pl.loop(0, NB)
    def _(i):
        @pl.loop(0, NF)
        def _(d):
            j = d * NB + i
            rows = pl.ds(pl.multiple_of(j * NB, NB), NB)
            for q in range(T // H):
                u = pre_v[q, rows, :]
                half = 0.5 * (1.0 + lax.erf(u * SQRT_HALF))
                send_a[j, :, q * H:(q + 1) * H] = (u * half).astype(BF16)
                pre_v[q, rows, :] = half + u * jnp.exp(-0.5 * u * u) * INV_ROOT_TWO_PI

        push_a(i)

    mine = pl.ds(pl.multiple_of(core * H, H), H)
    other = pl.ds(pl.multiple_of((1 - core) * H, H), H)

    def hop1(g):
        return pltpu.make_async_remote_copy(
            src_ref=s1_v.at[g], dst_ref=r1_v.at[g], send_sem=s1_sem.at[g], recv_sem=r1_sem.at[g],
            device_id=sibling, device_id_type=MESH)

    def hop2(g):
        return pltpu.make_async_remote_copy(
            src_ref=s2_v.at[g], dst_ref=r2_v.at[g], send_sem=s2_sem.at[g], recv_sem=r2_sem.at[g],
            device_id=across, device_id_type=MESH)

    def hop3(g):
        return pltpu.make_async_remote_copy(
            src_ref=grad_v.at[g, mine], dst_ref=grad_v.at[g, mine], send_sem=s3_sem.at[g], recv_sem=r3_sem.at[g],
            device_id=sibling, device_id_type=MESH)

    def first(g, value):
        keep_v[...] = value
        r2_own = keep_v[mine, :]
        s1_v[g] = keep_v[other, :]
        hop1(g).start()
        grad_v[g, mine] = r2_own

    def second(g):
        hop1(g).wait_recv()
        s2_v[g] = (grad_v[g, mine] + r1_v[g]).astype(BF16)
        hop2(g).start()

    norm = 1.0 / math.sqrt(T * 4)

    def third(g):
        hop2(g).wait_recv()
        grad_v[g, mine] = (s2_v[g].astype(F32) + r2_v[g].astype(F32)) * norm
        hop3(g).start()

    @pl.loop(0, NB)
    def _(i):
        pltpu.make_async_copy(send_d.at[i], send_d.at[i], rd_sem.at[i]).wait()

        @pl.loop(0, NF)
        def _(d):
            j = d * NB + i
            rows = pl.ds(pl.multiple_of(j * NB, NB), NB)
            for q in range(T // H):
                pre_v[q, rows, :] = pre_v[q, rows, :] * recv_d[j, :, q * H:(q + 1) * H].astype(F32)

    @pl.loop(0, NB)
    def _(b):
        g = jnp.concatenate(
            [pre_v[q, pl.ds(b, W, stride=NB), :].astype(BF16) for q in range(T // H)], axis=1)
        first(b, dot(g, x_v[b]).T)
        x_v[b] = dot(g, l_v[b], TT).astype(BF16)

        @pl.when(b >= 1)
        def _():
            second(b - 1)

    @pl.loop(0, NB)
    def _(i):
        pltpu.make_async_copy(send_d.at[i], send_d.at[i], ra_sem.at[i]).wait()
        a = recv_a[i].astype(F32).reshape(W, T).astype(BF16)
        first(NB + i, dot(a, c_v[i]))
        c_v[i] = dot(a, r_v[i], TN).astype(BF16)
        second(NB + i - 1)

    second(2 * NB - 1)

    @pl.loop(0, 2 * NB)
    def _(g):
        third(g)

    @pl.loop(0, 2 * NB)
    def _(g):
        hop3(g).wait_recv()
        hop1(g).wait_send()
        hop2(g).wait_send()
        hop3(g).wait_send()

    @pl.loop(0, NB)
    def _(i):
        pltpu.make_async_remote_copy(
            src_ref=send_d.at[i, pl.ds(0, NF - 1)], dst_ref=recv_d.at[pl.ds(0, NF - 1)],
            send_sem=sd_sem.at[i], recv_sem=rd_sem.at[i], device_id=sibling, device_id_type=MESH).wait_send()
        pltpu.make_async_remote_copy(
            src_ref=send_d.at[i, pl.ds(0, NF - 1)], dst_ref=recv_d.at[pl.ds(0, NF - 1)],
            send_sem=sa_sem.at[i], recv_sem=ra_sem.at[i], device_id=sibling, device_id_type=MESH).wait_send()


def write(out_v, ig_v, grad_v, out, ig, lg, rg, sem):
    copies = [
        pltpu.make_async_copy(grad_v.at[pl.ds(0, NB)], lg, sem.at[0]),
        pltpu.make_async_copy(grad_v.at[pl.ds(NB, NB)], rg, sem.at[1]),
    ]
    for n in range(NB):
        copies.append(pltpu.make_async_copy(out_v.at[n], out.at[:, n * W:(n + 1) * W], sem.at[2 + n]))
        copies.append(pltpu.make_async_copy(ig_v.at[n], ig.at[:, n * W:(n + 1) * W], sem.at[2 + NB + n]))
    for copy in copies:
        copy.start()
    for copy in copies:
        copy.wait()


def local(tokens, left_factor, right_factor, cotangent):
    any_spec = pl.BlockSpec(memory_space=pl.ANY)
    dma = pltpu.SemaphoreType.DMA
    vmem_spec = pl.BlockSpec(memory_space=pltpu.VMEM)
    held = pl.pallas_call(
        kernel,
        out_shape=(
            jax.ShapeDtypeStruct((NB, T, W), BF16),
            jax.ShapeDtypeStruct((NB, T, W), BF16),
            jax.ShapeDtypeStruct((2 * NB, W, W), F32),
        ),
        in_specs=[pl.BlockSpec(memory_space=pltpu.HBM)] * 4,
        out_specs=(vmem_spec,) * 3,
        scratch_shapes=[
            pltpu.VMEM((NB, W, W), BF16), pltpu.VMEM((NB, W, W), BF16),
            pltpu.VMEM((NB, NF, NB, T), BF16), pltpu.VMEM((NF * NB, NB, T), BF16),
            pltpu.VMEM((T // H, W * NB, H), F32),
            pltpu.VMEM((NF * NB, NB, T), BF16), pltpu.VMEM((NB, NF, NB, T), BF16),
            pltpu.VMEM((W, W), F32),
            pltpu.VMEM((2 * NB, H, W), F32), pltpu.VMEM((2 * NB, H, W), F32),
            pltpu.VMEM((2 * NB, H, W), BF16), pltpu.VMEM((2 * NB, H, W), BF16),
            dma((NB,)), dma((NB,)), dma((2,)), dma((NB,)), dma((NB,)), dma((NB,)), dma((NB,)),
            dma((2 * NB,)), dma((2 * NB,)), dma((2 * NB,)), dma((2 * NB,)), dma((2 * NB,)), dma((2 * NB,)),
        ],
        compiler_params=pltpu.CompilerParams(
            collective_id=0, has_side_effects=True, vmem_limit_bytes=36 << 20),
        name="monarch",
    )(*[pltpu.with_memory_space_constraint(v, pltpu.HBM) for v in (tokens, left_factor, right_factor, cotangent)])
    return pl.pallas_call(
        write,
        out_shape=(
            jax.ShapeDtypeStruct(tokens.shape, BF16),
            jax.ShapeDtypeStruct(tokens.shape, BF16),
            jax.ShapeDtypeStruct(left_factor.shape, F32),
            jax.ShapeDtypeStruct(right_factor.shape, F32),
        ),
        in_specs=[vmem_spec] * 3,
        out_specs=(any_spec,) * 4,
        scratch_shapes=[dma((2 + 2 * NB,))],
        compiler_params=pltpu.CompilerParams(vmem_limit_bytes=1 << 20),
        name="write",
    )(*held)


def solution(mesh):
    in_specs = (P("dp", "feat"), P("feat", None, None), P("feat", None, None), P("dp", "feat"))
    out_specs = (P("dp", "feat"), P("dp", "feat"), P("feat", None, None), P("feat", None, None))
    return jax.shard_map(local, mesh=mesh, in_specs=in_specs, out_specs=out_specs, check_vma=False)
```

```python
import math

import jax
import jax.numpy as jnp
from jax import lax
from jax.experimental import pallas as pl
from jax.experimental.pallas import tpu as pltpu
from jax.sharding import PartitionSpec as P

SQRT_HALF = 0.7071067811865476
INV_ROOT_TWO_PI = 0.3989422804014327
MESH = pl.DeviceIdType.MESH
F32 = jnp.float32
BF16 = jnp.bfloat16
NT = (((1,), (1,)), ((), ()))
TN = (((0,), (0,)), ((), ()))
TT = (((0,), (1,)), ((), ()))
NF = 32
NP = 16
NB = 8
T = 1024
W = 256
H = 128
ORDER = [(7 * k) % NP for k in range(1, NP)]
HOLD = 1


def dot(a, b, dims=(((1,), (0,)), ((), ()))):
    return lax.dot_general(a, b, dims, preferred_element_type=F32)


def kernel(
    tok, lf, rf, ct, c_v, x_v, grad_v,
    l_v, r_v, send_d, mid_d, recv_d, pre_v, send_a, mid_a, recv_a,
    keep_v, s1_v, r1_v, s2_v, r2_v,
    x_sem, c_sem, w_sem, sd_sem, yd_sem, md_sem, rd_sem, sa_sem, ya_sem, ma_sem, ra_sem,
    s1_sem, r1_sem, s2_sem, r2_sem, s3_sem, r3_sem,
):
    dp = lax.axis_index("dp")
    me = lax.axis_index("feat")
    core = dp % 2
    sibling = (dp + 1 - 2 * core, me)
    across = ((dp + 2) % 4, me)
    plane, spot = me // NP, me % NP
    flip = (1 - plane) * NP + spot
    peers = [((spot // 4 + p // 4) % 4) * 4 + (spot + p) % 4 for p in ORDER]

    def cols(n):
        return pl.ds(pl.multiple_of(n * W, W), W)

    def load_c(n):
        return pltpu.make_async_copy(ct.at[:, cols(n)], c_v.at[n], c_sem.at[n])

    def load_x(n):
        return pltpu.make_async_copy(tok.at[:, cols(n)], x_v.at[n], x_sem.at[n])

    load_r0 = pltpu.make_async_copy(rf.at[0], r_v.at[0], w_sem.at[2])
    load_r = pltpu.make_async_copy(rf.at[pl.ds(1, NB - 1)], r_v.at[pl.ds(1, NB - 1)], w_sem.at[0])
    load_l = pltpu.make_async_copy(lf, l_v, w_sem.at[1])
    load_r0.start()
    load_c(0).start()

    barrier = pltpu.get_barrier_semaphore()
    for d in [sibling, across, (dp, flip)] + [(dp, plane * NP + p) for p in peers]:
        pl.semaphore_signal(barrier, inc=1, device_id=d, device_id_type=MESH)

    load_r.start()

    @pl.loop(1, NB)
    def _(n):
        load_c(n).start()

    load_l.start()

    @pl.loop(0, NB)
    def _(n):
        load_x(n).start()

    def over(i, send, mid, ssem, rsem):
        return pltpu.make_async_remote_copy(
            src_ref=send.at[i, pl.ds((1 - plane) * NP, NP)], dst_ref=mid.at[i],
            send_sem=ssem.at[i], recv_sem=rsem.at[i], device_id=(dp, flip), device_id_type=MESH)

    def spread(src, dst, ssem, rsem):
        for p in peers:
            pltpu.make_async_remote_copy(
                src_ref=src(p), dst_ref=dst, send_sem=ssem, recv_sem=rsem,
                device_id=(dp, plane * NP + p), device_id_type=MESH).start()
        pltpu.make_async_copy(src(spot), dst, rsem).start()

    def over_d(i):
        return over(i, send_d, mid_d, yd_sem, md_sem)

    def own_d(i):
        spread(lambda p: send_d.at[i, plane * NP + p], recv_d.at[me * NB + i], sd_sem.at[i], rd_sem.at[i])

    def forward_d(i):
        over_d(i).wait_recv()
        spread(lambda p: mid_d.at[i, p], recv_d.at[flip * NB + i], sd_sem.at[i], rd_sem.at[i])

    def over_a(i):
        return over(i, send_a, mid_a, ya_sem, ma_sem)

    def own_a(i):
        spread(lambda p: send_a.at[i, plane * NP + p], recv_a.at[i, me], sa_sem.at[i], ra_sem.at[i])

    def forward_a(i):
        over_a(i).wait_recv()
        spread(lambda p: mid_a.at[i, p], recv_a.at[i, flip], sa_sem.at[i], ra_sem.at[i])

    def compute_d(i):
        load_c(i).wait()
        v = dot(r_v[i], c_v[i], NT)
        send_d[i] = v.reshape(NF, NB, T).astype(BF16)

    load_r0.wait()
    compute_d(0)
    pl.semaphore_wait(barrier, NP + 2)
    over_d(0).start()
    own_d(0)
    load_r.wait()

    @pl.loop(1, NB)
    def _(i):
        compute_d(i)
        over_d(i).start()
        own_d(i)

    load_l.wait()

    @pl.loop(0, NB)
    def _(b):
        load_x(b).wait()
        v = dot(l_v[b], x_v[b], TT)
        for q in range(T // H):
            pre_v[q, pl.ds(b, W, stride=NB), :] = v[:, q * H:(q + 1) * H]

        @pl.when(b % 2 == 1)
        def _():
            forward_d(b // 2)

    @pl.loop(0, NB)
    def _(i):
        @pl.loop(0, NF)
        def _(d):
            j = d * NB + i
            rows = pl.ds(pl.multiple_of(j * NB, NB), NB)
            for q in range(T // H):
                u = pre_v[q, rows, :]
                half = 0.5 * (1.0 + lax.erf(u * SQRT_HALF))
                send_a[i, d, :, q * H:(q + 1) * H] = (u * half).astype(BF16)
                pre_v[q, rows, :] = half + u * jnp.exp(-0.5 * u * u) * INV_ROOT_TWO_PI

        over_a(i).start()
        own_a(i)

        @pl.when(i % 2 == 1)
        def _():
            forward_d(NB // 2 + i // 2)

    mine = pl.ds(pl.multiple_of(core * H, H), H)
    other = pl.ds(pl.multiple_of((1 - core) * H, H), H)

    def hop1(g):
        return pltpu.make_async_remote_copy(
            src_ref=s1_v.at[g], dst_ref=r1_v.at[g], send_sem=s1_sem.at[g], recv_sem=r1_sem.at[g],
            device_id=sibling, device_id_type=MESH)

    def hop2(g):
        return pltpu.make_async_remote_copy(
            src_ref=s2_v.at[g], dst_ref=r2_v.at[g], send_sem=s2_sem.at[g], recv_sem=r2_sem.at[g],
            device_id=across, device_id_type=MESH)

    def hop3(g):
        return pltpu.make_async_remote_copy(
            src_ref=grad_v.at[g, mine], dst_ref=grad_v.at[g, mine], send_sem=s3_sem.at[g], recv_sem=r3_sem.at[g],
            device_id=sibling, device_id_type=MESH)

    def first(g, value):
        keep_v[...] = value
        r2_own = keep_v[mine, :]
        s1_v[g] = keep_v[other, :]
        hop1(g).start()
        grad_v[g, mine] = r2_own

    def second(g):
        hop1(g).wait_recv()
        s2_v[g] = (grad_v[g, mine] + r1_v[g]).astype(BF16)
        hop2(g).start()

    norm = 1.0 / math.sqrt(T * 4)

    def third(g):
        hop2(g).wait_recv()
        grad_v[g, mine] = (s2_v[g].astype(F32) + r2_v[g].astype(F32)) * norm
        hop3(g).start()

    @pl.loop(0, NB)
    def _(i):
        pltpu.make_async_copy(send_d.at[i], send_d.at[i], rd_sem.at[i]).wait()

        @pl.loop(0, NF)
        def _(d):
            j = d * NB + i
            rows = pl.ds(pl.multiple_of(j * NB, NB), NB)
            for q in range(T // H):
                pre_v[q, rows, :] = pre_v[q, rows, :] * recv_d[j, :, q * H:(q + 1) * H].astype(F32)

    @pl.loop(0, NB)
    def _(b):
        g = jnp.concatenate(
            [pre_v[q, pl.ds(b, W, stride=NB), :].astype(BF16) for q in range(T // H)], axis=1)
        first(b, dot(g, x_v[b]).T)
        x_v[b] = dot(g, l_v[b], TT).astype(BF16)

        @pl.when(b % 2 == 1)
        def _():
            forward_a(b // 2)

    @pl.loop(0, NB)
    def _(i):
        pltpu.make_async_copy(send_d.at[i], send_d.at[i], ra_sem.at[i]).wait()
        a = recv_a[i].astype(F32).reshape(W, T).astype(BF16)
        first(NB + i, dot(a, c_v[i]))
        c_v[i] = dot(a, r_v[i], TN).astype(BF16)

        @pl.when(i < NB // 2)
        def _():
            forward_a(NB // 2 + i)

        @pl.when(i == HOLD)
        def _():
            @pl.loop(0, NB + HOLD)
            def _(g):
                second(g)

        @pl.when(i > HOLD)
        def _():
            second(NB + i - 1)

    second(2 * NB - 1)

    @pl.loop(0, NB)
    def _(i):
        for over_x, sem in ((over_d, sd_sem), (over_a, sa_sem)):
            over_x(i).wait_send()
            pltpu.make_async_remote_copy(
                src_ref=send_d.at[i, pl.ds(0, NF - 2)], dst_ref=recv_d.at[pl.ds(0, NF - 2)],
                send_sem=sem.at[i], recv_sem=rd_sem.at[i], device_id=sibling, device_id_type=MESH).wait_send()

    @pl.loop(0, 2 * NB)
    def _(g):
        hop1(g).wait_send()
        third(g)
        hop2(g).wait_send()

        @pl.when(g >= 2)
        def _():
            hop3(g - 2).wait()

    for g in (2 * NB - 2, 2 * NB - 1):
        hop3(g).wait()


def write(out_v, ig_v, grad_v, out, ig, lg, rg, sem):
    copies = [
        pltpu.make_async_copy(grad_v.at[pl.ds(0, NB)], lg, sem.at[0]),
        pltpu.make_async_copy(grad_v.at[pl.ds(NB, NB)], rg, sem.at[1]),
    ]
    for n in range(NB):
        copies.append(pltpu.make_async_copy(out_v.at[n], out.at[:, n * W:(n + 1) * W], sem.at[2 + n]))
        copies.append(pltpu.make_async_copy(ig_v.at[n], ig.at[:, n * W:(n + 1) * W], sem.at[2 + NB + n]))
    for copy in copies:
        copy.start()
    for copy in copies:
        copy.wait()


def local(tokens, left_factor, right_factor, cotangent):
    any_spec = pl.BlockSpec(memory_space=pl.ANY)
    dma = pltpu.SemaphoreType.DMA
    vmem_spec = pl.BlockSpec(memory_space=pltpu.VMEM)
    held = pl.pallas_call(
        kernel,
        out_shape=(
            jax.ShapeDtypeStruct((NB, T, W), BF16),
            jax.ShapeDtypeStruct((NB, T, W), BF16),
            jax.ShapeDtypeStruct((2 * NB, W, W), F32),
        ),
        in_specs=[pl.BlockSpec(memory_space=pltpu.HBM)] * 4,
        out_specs=(vmem_spec,) * 3,
        scratch_shapes=[
            pltpu.VMEM((NB, W, W), BF16), pltpu.VMEM((NB, W, W), BF16),
            pltpu.VMEM((NB, NF, NB, T), BF16), pltpu.VMEM((NB, NP, NB, T), BF16), pltpu.VMEM((NF * NB, NB, T), BF16),
            pltpu.VMEM((T // H, W * NB, H), F32),
            pltpu.VMEM((NB, NF, NB, T), BF16), pltpu.VMEM((NB, NP, NB, T), BF16), pltpu.VMEM((NB, NF, NB, T), BF16),
            pltpu.VMEM((W, W), F32),
            pltpu.VMEM((2 * NB, H, W), F32), pltpu.VMEM((2 * NB, H, W), F32),
            pltpu.VMEM((2 * NB, H, W), BF16), pltpu.VMEM((2 * NB, H, W), BF16),
            dma((NB,)), dma((NB,)), dma((3,)), *[dma((NB,))] * 8,
            dma((2 * NB,)), dma((2 * NB,)), dma((2 * NB,)), dma((2 * NB,)), dma((2 * NB,)), dma((2 * NB,)),
        ],
        compiler_params=pltpu.CompilerParams(
            collective_id=0, has_side_effects=True, vmem_limit_bytes=40 << 20),
        name="monarch",
    )(*[pltpu.with_memory_space_constraint(v, pltpu.HBM) for v in (tokens, left_factor, right_factor, cotangent)])
    return pl.pallas_call(
        write,
        out_shape=(
            jax.ShapeDtypeStruct(tokens.shape, BF16),
            jax.ShapeDtypeStruct(tokens.shape, BF16),
            jax.ShapeDtypeStruct(left_factor.shape, F32),
            jax.ShapeDtypeStruct(right_factor.shape, F32),
        ),
        in_specs=[vmem_spec] * 3,
        out_specs=(any_spec,) * 4,
        scratch_shapes=[dma((2 + 2 * NB,))],
        compiler_params=pltpu.CompilerParams(vmem_limit_bytes=1 << 20),
        name="write",
    )(*held)


def solution(mesh):
    in_specs = (P("dp", "feat"), P("feat", None, None), P("feat", None, None), P("dp", "feat"))
    out_specs = (P("dp", "feat"), P("dp", "feat"), P("feat", None, None), P("feat", None, None))
    return jax.shard_map(local, mesh=mesh, in_specs=in_specs, out_specs=out_specs, check_vma=False)
```

```python
import math

import jax
import jax.numpy as jnp
from jax import lax
from jax.experimental import pallas as pl
from jax.experimental.pallas import tpu as pltpu
from jax.sharding import PartitionSpec as P

SQRT_HALF = 0.7071067811865476
INV_ROOT_TWO_PI = 0.3989422804014327
MESH = pl.DeviceIdType.MESH
F32 = jnp.float32
BF16 = jnp.bfloat16
NT = (((1,), (1,)), ((), ()))
TN = (((0,), (0,)), ((), ()))
TT = (((0,), (1,)), ((), ()))
NF = 32
NP = 16
NB = 8
T = 1024
W = 256
H = 128
ORDER = [(7 * k) % NP for k in range(1, NP)]
LAG = 5


def dot(a, b, dims=(((1,), (0,)), ((), ()))):
    return lax.dot_general(a, b, dims, preferred_element_type=F32)


def kernel(
    tok, lf, rf, ct, c_v, x_v, grad_v,
    l_v, r_v, send_d, mid_d, recv_d, pre_v, send_a, mid_a, recv_a,
    keep_v, s1_v, r1_v, s2_v, r2_v,
    x_sem, c_sem, w_sem, sd_sem, yd_sem, md_sem, rd_sem, sa_sem, ya_sem, ma_sem, ra_sem,
    s1_sem, r1_sem, s2_sem, r2_sem, s3_sem, r3_sem,
):
    dp = lax.axis_index("dp")
    me = lax.axis_index("feat")
    core = dp % 2
    sibling = (dp + 1 - 2 * core, me)
    across = ((dp + 2) % 4, me)
    plane, spot = me // NP, me % NP
    flip = (1 - plane) * NP + spot
    peers = [((spot // 4 + p // 4) % 4) * 4 + (spot + p) % 4 for p in ORDER]

    def cols(n):
        return pl.ds(pl.multiple_of(n * W, W), W)

    def load_c(n):
        return pltpu.make_async_copy(ct.at[:, cols(n)], c_v.at[n], c_sem.at[n])

    def load_x(n):
        return pltpu.make_async_copy(tok.at[:, cols(n)], x_v.at[n], x_sem.at[n])

    load_r0 = pltpu.make_async_copy(rf.at[0], r_v.at[0], w_sem.at[2])
    load_r = pltpu.make_async_copy(rf.at[pl.ds(1, NB - 1)], r_v.at[pl.ds(1, NB - 1)], w_sem.at[0])
    load_l = pltpu.make_async_copy(lf, l_v, w_sem.at[1])
    load_r0.start()
    load_c(0).start()

    barrier = pltpu.get_barrier_semaphore()
    for d in [sibling, across, (dp, flip)] + [(dp, plane * NP + p) for p in peers]:
        pl.semaphore_signal(barrier, inc=1, device_id=d, device_id_type=MESH)

    load_r.start()

    @pl.loop(1, NB)
    def _(n):
        load_c(n).start()

    load_l.start()

    @pl.loop(0, NB)
    def _(n):
        load_x(n).start()

    def over(i, send, mid, ssem, rsem):
        return pltpu.make_async_remote_copy(
            src_ref=send.at[i, pl.ds((1 - plane) * NP, NP)], dst_ref=mid.at[i],
            send_sem=ssem.at[i], recv_sem=rsem.at[i], device_id=(dp, flip), device_id_type=MESH)

    def spread(src, dst, ssem, rsem):
        for p in peers:
            pltpu.make_async_remote_copy(
                src_ref=src(p), dst_ref=dst, send_sem=ssem, recv_sem=rsem,
                device_id=(dp, plane * NP + p), device_id_type=MESH).start()
        pltpu.make_async_copy(src(spot), dst, rsem).start()

    def over_d(i):
        return over(i, send_d, mid_d, yd_sem, md_sem)

    def own_d(i):
        spread(lambda p: send_d.at[i, plane * NP + p], recv_d.at[me * NB + i], sd_sem.at[i], rd_sem.at[i])

    def forward_d(i):
        over_d(i).wait_recv()
        spread(lambda p: mid_d.at[i, p], recv_d.at[flip * NB + i], sd_sem.at[i], rd_sem.at[i])

    def over_a(i):
        return over(i, send_a, mid_a, ya_sem, ma_sem)

    def own_a(i):
        spread(lambda p: send_a.at[i, plane * NP + p], recv_a.at[i, me], sa_sem.at[i], ra_sem.at[i])

    def forward_a(i):
        over_a(i).wait_recv()
        spread(lambda p: mid_a.at[i, p], recv_a.at[i, flip], sa_sem.at[i], ra_sem.at[i])

    def compute_d(i):
        load_c(i).wait()
        v = dot(r_v[i], c_v[i], NT)
        send_d[i] = v.reshape(NF, NB, T).astype(BF16)

    load_r0.wait()
    compute_d(0)
    pl.semaphore_wait(barrier, NP + 2)
    over_d(0).start()
    own_d(0)
    load_r.wait()

    @pl.loop(1, NB)
    def _(i):
        compute_d(i)
        over_d(i).start()
        own_d(i)

    load_l.wait()

    @pl.loop(0, NB)
    def _(b):
        load_x(b).wait()
        v = dot(l_v[b], x_v[b], TT)
        for q in range(T // H):
            pre_v[q, pl.ds(b, W, stride=NB), :] = v[:, q * H:(q + 1) * H]

        @pl.when(b % 2 == 1)
        def _():
            forward_d(b // 2)

    @pl.loop(0, NB)
    def _(i):
        @pl.loop(0, NF)
        def _(d):
            j = d * NB + i
            rows = pl.ds(pl.multiple_of(j * NB, NB), NB)
            for q in range(T // H):
                u = pre_v[q, rows, :]
                half = 0.5 * (1.0 + lax.erf(u * SQRT_HALF))
                send_a[i, d, :, q * H:(q + 1) * H] = (u * half).astype(BF16)
                pre_v[q, rows, :] = half + u * jnp.exp(-0.5 * u * u) * INV_ROOT_TWO_PI

        over_a(i).start()
        own_a(i)

        @pl.when(i % 2 == 1)
        def _():
            forward_d(NB // 2 + i // 2)

    mine = pl.ds(pl.multiple_of(core * H, H), H)
    other = pl.ds(pl.multiple_of((1 - core) * H, H), H)

    def hop1(g):
        return pltpu.make_async_remote_copy(
            src_ref=s1_v.at[g], dst_ref=r1_v.at[g], send_sem=s1_sem.at[g], recv_sem=r1_sem.at[g],
            device_id=sibling, device_id_type=MESH)

    def hop2(g):
        return pltpu.make_async_remote_copy(
            src_ref=s2_v.at[g], dst_ref=r2_v.at[g], send_sem=s2_sem.at[g], recv_sem=r2_sem.at[g],
            device_id=across, device_id_type=MESH)

    def hop3(g):
        return pltpu.make_async_remote_copy(
            src_ref=grad_v.at[g, mine], dst_ref=grad_v.at[g, mine], send_sem=s3_sem.at[g], recv_sem=r3_sem.at[g],
            device_id=sibling, device_id_type=MESH)

    def first(g, value):
        keep_v[...] = value
        r2_own = keep_v[mine, :]
        s1_v[g] = keep_v[other, :]
        hop1(g).start()
        grad_v[g, mine] = r2_own

    def second(g):
        hop1(g).wait_recv()
        s2_v[g] = (grad_v[g, mine] + r1_v[g]).astype(BF16)
        hop2(g).start()

    norm = 1.0 / math.sqrt(T * 4)

    def third(g):
        hop2(g).wait_recv()
        grad_v[g, mine] = (s2_v[g].astype(F32) + r2_v[g].astype(F32)) * norm
        hop3(g).start()

    @pl.loop(0, NB)
    def _(i):
        pltpu.make_async_copy(send_d.at[i], send_d.at[i], rd_sem.at[i]).wait()

        @pl.loop(0, NF)
        def _(d):
            j = d * NB + i
            rows = pl.ds(pl.multiple_of(j * NB, NB), NB)
            for q in range(T // H):
                pre_v[q, rows, :] = pre_v[q, rows, :] * recv_d[j, :, q * H:(q + 1) * H].astype(F32)

    @pl.loop(0, NB)
    def _(b):
        g = jnp.concatenate(
            [pre_v[q, pl.ds(b, W, stride=NB), :].astype(BF16) for q in range(T // H)], axis=1)
        first(b, dot(g, x_v[b]).T)
        x_v[b] = dot(g, l_v[b], TT).astype(BF16)

        @pl.when(b % 2 == 1)
        def _():
            forward_a(b // 2)

    @pl.loop(0, NB)
    def _(i):
        pltpu.make_async_copy(send_d.at[i], send_d.at[i], ra_sem.at[i]).wait()
        a = recv_a[i].astype(F32).reshape(W, T).astype(BF16)
        first(NB + i, dot(a, c_v[i]))
        c_v[i] = dot(a, r_v[i], TN).astype(BF16)

        @pl.when(i < NB // 2)
        def _():
            forward_a(NB // 2 + i)

        second(2 * i)

        @pl.when(i < NB - 1)
        def _():
            second(2 * i + 1)

        @pl.when(i >= LAG)
        def _():
            third(2 * (i - LAG))
            third(2 * (i - LAG) + 1)

    second(2 * NB - 1)

    @pl.loop(0, NB)
    def _(i):
        for over_x, sem in ((over_d, sd_sem), (over_a, sa_sem)):
            over_x(i).wait_send()
            pltpu.make_async_remote_copy(
                src_ref=send_d.at[i, pl.ds(0, NF - 2)], dst_ref=recv_d.at[pl.ds(0, NF - 2)],
                send_sem=sem.at[i], recv_sem=rd_sem.at[i], device_id=sibling, device_id_type=MESH).wait_send()

    @pl.loop(0, 2 * NB)
    def _(g):
        hop1(g).wait_send()

    @pl.loop(0, 2 * (NB - LAG))
    def _(g):
        hop3(g).wait()
        hop2(g).wait_send()

    for g in range(2 * (NB - LAG), 2 * NB):
        third(g)

    for g in range(2 * (NB - LAG), 2 * NB):
        hop2(g).wait_send()
        hop3(g).wait()


def write(out_v, ig_v, grad_v, out, ig, lg, rg, sem):
    copies = [
        pltpu.make_async_copy(grad_v.at[pl.ds(0, NB)], lg, sem.at[0]),
        pltpu.make_async_copy(grad_v.at[pl.ds(NB, NB)], rg, sem.at[1]),
    ]
    for n in range(NB):
        copies.append(pltpu.make_async_copy(out_v.at[n], out.at[:, n * W:(n + 1) * W], sem.at[2 + n]))
        copies.append(pltpu.make_async_copy(ig_v.at[n], ig.at[:, n * W:(n + 1) * W], sem.at[2 + NB + n]))
    for copy in copies:
        copy.start()
    for copy in copies:
        copy.wait()


def local(tokens, left_factor, right_factor, cotangent):
    any_spec = pl.BlockSpec(memory_space=pl.ANY)
    dma = pltpu.SemaphoreType.DMA
    vmem_spec = pl.BlockSpec(memory_space=pltpu.VMEM)
    held = pl.pallas_call(
        kernel,
        out_shape=(
            jax.ShapeDtypeStruct((NB, T, W), BF16),
            jax.ShapeDtypeStruct((NB, T, W), BF16),
            jax.ShapeDtypeStruct((2 * NB, W, W), F32),
        ),
        in_specs=[pl.BlockSpec(memory_space=pltpu.HBM)] * 4,
        out_specs=(vmem_spec,) * 3,
        scratch_shapes=[
            pltpu.VMEM((NB, W, W), BF16), pltpu.VMEM((NB, W, W), BF16),
            pltpu.VMEM((NB, NF, NB, T), BF16), pltpu.VMEM((NB, NP, NB, T), BF16), pltpu.VMEM((NF * NB, NB, T), BF16),
            pltpu.VMEM((T // H, W * NB, H), F32),
            pltpu.VMEM((NB, NF, NB, T), BF16), pltpu.VMEM((NB, NP, NB, T), BF16), pltpu.VMEM((NB, NF, NB, T), BF16),
            pltpu.VMEM((W, W), F32),
            pltpu.VMEM((2 * NB, H, W), F32), pltpu.VMEM((2 * NB, H, W), F32),
            pltpu.VMEM((2 * NB, H, W), BF16), pltpu.VMEM((2 * NB, H, W), BF16),
            dma((NB,)), dma((NB,)), dma((3,)), *[dma((NB,))] * 8,
            dma((2 * NB,)), dma((2 * NB,)), dma((2 * NB,)), dma((2 * NB,)), dma((2 * NB,)), dma((2 * NB,)),
        ],
        compiler_params=pltpu.CompilerParams(
            collective_id=0, has_side_effects=True, vmem_limit_bytes=40 << 20),
        name="monarch",
    )(*[pltpu.with_memory_space_constraint(v, pltpu.HBM) for v in (tokens, left_factor, right_factor, cotangent)])
    return pl.pallas_call(
        write,
        out_shape=(
            jax.ShapeDtypeStruct(tokens.shape, BF16),
            jax.ShapeDtypeStruct(tokens.shape, BF16),
            jax.ShapeDtypeStruct(left_factor.shape, F32),
            jax.ShapeDtypeStruct(right_factor.shape, F32),
        ),
        in_specs=[vmem_spec] * 3,
        out_specs=(any_spec,) * 4,
        scratch_shapes=[dma((2 + 2 * NB,))],
        compiler_params=pltpu.CompilerParams(vmem_limit_bytes=1 << 20),
        name="write",
    )(*held)


def solution(mesh):
    in_specs = (P("dp", "feat"), P("feat", None, None), P("feat", None, None), P("dp", "feat"))
    out_specs = (P("dp", "feat"), P("dp", "feat"), P("feat", None, None), P("feat", None, None))
    return jax.shard_map(local, mesh=mesh, in_specs=in_specs, out_specs=out_specs, check_vma=False)
```

```python
import math

import jax
import jax.numpy as jnp
from jax import lax
from jax.experimental import pallas as pl
from jax.experimental.pallas import tpu as pltpu
from jax.sharding import PartitionSpec as P

SQRT_HALF = 0.7071067811865476
INV_ROOT_TWO_PI = 0.3989422804014327
MESH = pl.DeviceIdType.MESH
F32 = jnp.float32
BF16 = jnp.bfloat16
NT = (((1,), (1,)), ((), ()))
TN = (((0,), (0,)), ((), ()))
TT = (((0,), (1,)), ((), ()))
NF = 32
NP = 16
NB = 8
T = 1024
W = 256
H = 128
ORDER = [(7 * k) % NP for k in range(1, NP)]
LAG = 5


def dot(a, b, dims=(((1,), (0,)), ((), ()))):
    return lax.dot_general(a, b, dims, preferred_element_type=F32)


def kernel(
    tok, lf, rf, ct, c_v, x_v, grad_v,
    l_v, r_v, send_d, mid_d, recv_d, pre_v, send_a, mid_a, recv_a,
    keep_v, s1_v, r1_v, s2_v, r2_v,
    x_sem, c_sem, w_sem, sd_sem, yd_sem, md_sem, rd_sem, sa_sem, ya_sem, ma_sem, ra_sem,
    s1_sem, r1_sem, s2_sem, r2_sem, s3_sem, r3_sem,
):
    dp = lax.axis_index("dp")
    me = lax.axis_index("feat")
    core = dp % 2
    sibling = (dp + 1 - 2 * core, me)
    across = ((dp + 2) % 4, me)
    plane, spot = me // NP, me % NP
    flip = (1 - plane) * NP + spot
    peers = [((spot // 4 + p // 4) % 4) * 4 + (spot + p) % 4 for p in ORDER]

    def cols(n):
        return pl.ds(pl.multiple_of(n * W, W), W)

    def load_c(n):
        return pltpu.make_async_copy(ct.at[:, cols(n)], c_v.at[n], c_sem.at[n])

    def load_x(n):
        return pltpu.make_async_copy(tok.at[:, cols(n)], x_v.at[n], x_sem.at[n])

    load_r0 = pltpu.make_async_copy(rf.at[0], r_v.at[0], w_sem.at[2])
    load_r = pltpu.make_async_copy(rf.at[pl.ds(1, NB - 1)], r_v.at[pl.ds(1, NB - 1)], w_sem.at[0])
    load_l = pltpu.make_async_copy(lf, l_v, w_sem.at[1])
    load_r0.start()
    load_c(0).start()

    barrier = pltpu.get_barrier_semaphore()
    for d in [sibling, across, (dp, flip)] + [(dp, plane * NP + p) for p in peers]:
        pl.semaphore_signal(barrier, inc=1, device_id=d, device_id_type=MESH)

    load_r.start()

    @pl.loop(1, NB)
    def _(n):
        load_c(n).start()

    load_l.start()

    @pl.loop(0, NB)
    def _(n):
        load_x(n).start()

    def over(i, send, mid, ssem, rsem):
        return pltpu.make_async_remote_copy(
            src_ref=send.at[i, pl.ds((1 - plane) * NP, NP)], dst_ref=mid.at[i],
            send_sem=ssem.at[i], recv_sem=rsem.at[i], device_id=(dp, flip), device_id_type=MESH)

    def spread(src, dst, ssem, rsem):
        for p in peers:
            pltpu.make_async_remote_copy(
                src_ref=src(p), dst_ref=dst, send_sem=ssem, recv_sem=rsem,
                device_id=(dp, plane * NP + p), device_id_type=MESH).start()
        pltpu.make_async_copy(src(spot), dst, rsem).start()

    def over_d(i):
        return over(i, send_d, mid_d, yd_sem, md_sem)

    def own_d(i):
        spread(lambda p: send_d.at[i, plane * NP + p], recv_d.at[me * NB + i], sd_sem.at[i], rd_sem.at[i])

    def forward_d(i):
        over_d(i).wait_recv()
        spread(lambda p: mid_d.at[i, p], recv_d.at[flip * NB + i], sd_sem.at[i], rd_sem.at[i])

    def over_a(i):
        return over(i, send_a, mid_a, ya_sem, ma_sem)

    def own_a(i):
        spread(lambda p: send_a.at[i, plane * NP + p], recv_a.at[i, me], sa_sem.at[i], ra_sem.at[i])

    def forward_a(i):
        over_a(i).wait_recv()
        spread(lambda p: mid_a.at[i, p], recv_a.at[i, flip], sa_sem.at[i], ra_sem.at[i])

    def compute_d(i):
        load_c(i).wait()
        v = dot(r_v[i], c_v[i], NT)
        send_d[i] = v.reshape(NF, NB, T).astype(BF16)

    load_r0.wait()
    compute_d(0)
    pl.semaphore_wait(barrier, NP + 2)
    over_d(0).start()
    own_d(0)
    load_r.wait()

    @pl.loop(1, NB)
    def _(i):
        compute_d(i)
        over_d(i).start()
        own_d(i)

    load_l.wait()

    @pl.loop(0, NB)
    def _(b):
        load_x(b).wait()
        v = dot(l_v[b], x_v[b], TT)
        for q in range(T // H):
            pre_v[q, pl.ds(b, W, stride=NB), :] = v[:, q * H:(q + 1) * H]

        @pl.when(b % 2 == 1)
        def _():
            forward_d(b // 2)

    @pl.loop(0, NB)
    def _(i):
        @pl.loop(0, NF)
        def _(d):
            j = d * NB + i
            rows = pl.ds(pl.multiple_of(j * NB, NB), NB)
            for q in range(T // H):
                u = pre_v[q, rows, :]
                half = 0.5 * (1.0 + lax.erf(u * SQRT_HALF))
                send_a[i, d, :, q * H:(q + 1) * H] = (u * half).astype(BF16)
                pre_v[q, rows, :] = half + u * jnp.exp(-0.5 * u * u) * INV_ROOT_TWO_PI

        over_a(i).start()
        own_a(i)

        @pl.when(i % 2 == 1)
        def _():
            forward_d(NB // 2 + i // 2)

    mine = pl.ds(pl.multiple_of(core * H, H), H)
    other = pl.ds(pl.multiple_of((1 - core) * H, H), H)

    def hop1(g):
        return pltpu.make_async_remote_copy(
            src_ref=s1_v.at[g], dst_ref=r1_v.at[g], send_sem=s1_sem.at[g], recv_sem=r1_sem.at[g],
            device_id=sibling, device_id_type=MESH)

    def hop2(g):
        return pltpu.make_async_remote_copy(
            src_ref=s2_v.at[g], dst_ref=r2_v.at[g], send_sem=s2_sem.at[g], recv_sem=r2_sem.at[g],
            device_id=across, device_id_type=MESH)

    def hop3(g):
        return pltpu.make_async_remote_copy(
            src_ref=grad_v.at[g, mine], dst_ref=grad_v.at[g, mine], send_sem=s3_sem.at[g], recv_sem=r3_sem.at[g],
            device_id=sibling, device_id_type=MESH)

    def first(g, value):
        keep_v[...] = value
        r2_own = keep_v[mine, :]
        s1_v[g] = keep_v[other, :]
        hop1(g).start()
        grad_v[g, mine] = r2_own

    def second(g):
        hop1(g).wait_recv()
        s2_v[g] = (grad_v[g, mine] + r1_v[g]).astype(BF16)
        hop2(g).start()

    norm = 1.0 / math.sqrt(T * 4)

    def third(g):
        hop2(g).wait_recv()
        grad_v[g, mine] = (s2_v[g].astype(F32) + r2_v[g].astype(F32)) * norm
        hop3(g).start()

    @pl.loop(0, NB)
    def _(i):
        pltpu.make_async_copy(send_d.at[i], send_d.at[i], rd_sem.at[i]).wait()

        @pl.loop(0, NF)
        def _(d):
            j = d * NB + i
            rows = pl.ds(pl.multiple_of(j * NB, NB), NB)
            for q in range(T // H):
                pre_v[q, rows, :] = pre_v[q, rows, :] * recv_d[j, :, q * H:(q + 1) * H].astype(F32)

    @pl.loop(0, NB)
    def _(b):
        g = jnp.concatenate(
            [pre_v[q, pl.ds(b, W, stride=NB), :].astype(BF16) for q in range(T // H)], axis=1)
        first(b, dot(g, x_v[b]).T)
        x_v[b] = dot(g, l_v[b], TT).astype(BF16)

        @pl.when(b % 2 == 1)
        def _():
            forward_a(b // 2)

    @pl.loop(0, NB)
    def _(i):
        pltpu.make_async_copy(send_d.at[i], send_d.at[i], ra_sem.at[i]).wait()
        a = recv_a[i].astype(F32).reshape(W, T).astype(BF16)
        first(NB + i, dot(a, c_v[i]))
        c_v[i] = dot(a, r_v[i], TN).astype(BF16)

        @pl.when(i < NB // 2)
        def _():
            forward_a(NB // 2 + i)

        second(2 * i)
        second(2 * i + 1)

        @pl.when(i >= LAG)
        def _():
            third(2 * (i - LAG))
            third(2 * (i - LAG) + 1)

    @pl.loop(0, NB)
    def _(i):
        for over_x, sem in ((over_d, sd_sem), (over_a, sa_sem)):
            over_x(i).wait_send()
            pltpu.make_async_remote_copy(
                src_ref=send_d.at[i, pl.ds(0, NF - 2)], dst_ref=recv_d.at[pl.ds(0, NF - 2)],
                send_sem=sem.at[i], recv_sem=rd_sem.at[i], device_id=sibling, device_id_type=MESH).wait_send()

    @pl.loop(0, 2 * NB)
    def _(g):
        hop1(g).wait_send()

    @pl.loop(0, 2 * (NB - LAG))
    def _(g):
        hop3(g).wait()
        hop2(g).wait_send()

    for g in range(2 * (NB - LAG), 2 * NB):
        third(g)

    for g in range(2 * (NB - LAG), 2 * NB):
        hop2(g).wait_send()
        hop3(g).wait()


def write(out_v, ig_v, grad_v, out, ig, lg, rg, sem):
    copies = [
        pltpu.make_async_copy(grad_v.at[pl.ds(0, NB)], lg, sem.at[0]),
        pltpu.make_async_copy(grad_v.at[pl.ds(NB, NB)], rg, sem.at[1]),
    ]
    for n in range(NB):
        copies.append(pltpu.make_async_copy(out_v.at[n], out.at[:, n * W:(n + 1) * W], sem.at[2 + n]))
        copies.append(pltpu.make_async_copy(ig_v.at[n], ig.at[:, n * W:(n + 1) * W], sem.at[2 + NB + n]))
    for copy in copies:
        copy.start()
    for copy in copies:
        copy.wait()


def local(tokens, left_factor, right_factor, cotangent):
    any_spec = pl.BlockSpec(memory_space=pl.ANY)
    dma = pltpu.SemaphoreType.DMA
    vmem_spec = pl.BlockSpec(memory_space=pltpu.VMEM)
    held = pl.pallas_call(
        kernel,
        out_shape=(
            jax.ShapeDtypeStruct((NB, T, W), BF16),
            jax.ShapeDtypeStruct((NB, T, W), BF16),
            jax.ShapeDtypeStruct((2 * NB, W, W), F32),
        ),
        in_specs=[pl.BlockSpec(memory_space=pltpu.HBM)] * 4,
        out_specs=(vmem_spec,) * 3,
        scratch_shapes=[
            pltpu.VMEM((NB, W, W), BF16), pltpu.VMEM((NB, W, W), BF16),
            pltpu.VMEM((NB, NF, NB, T), BF16), pltpu.VMEM((NB, NP, NB, T), BF16), pltpu.VMEM((NF * NB, NB, T), BF16),
            pltpu.VMEM((T // H, W * NB, H), F32),
            pltpu.VMEM((NB, NF, NB, T), BF16), pltpu.VMEM((NB, NP, NB, T), BF16), pltpu.VMEM((NB, NF, NB, T), BF16),
            pltpu.VMEM((W, W), F32),
            pltpu.VMEM((2 * NB, H, W), F32), pltpu.VMEM((2 * NB, H, W), F32),
            pltpu.VMEM((2 * NB, H, W), BF16), pltpu.VMEM((2 * NB, H, W), BF16),
            dma((NB,)), dma((NB,)), dma((3,)), *[dma((NB,))] * 8,
            dma((2 * NB,)), dma((2 * NB,)), dma((2 * NB,)), dma((2 * NB,)), dma((2 * NB,)), dma((2 * NB,)),
        ],
        compiler_params=pltpu.CompilerParams(
            collective_id=0, has_side_effects=True, vmem_limit_bytes=40 << 20),
        name="monarch",
    )(*[pltpu.with_memory_space_constraint(v, pltpu.HBM) for v in (tokens, left_factor, right_factor, cotangent)])
    return pl.pallas_call(
        write,
        out_shape=(
            jax.ShapeDtypeStruct(tokens.shape, BF16),
            jax.ShapeDtypeStruct(tokens.shape, BF16),
            jax.ShapeDtypeStruct(left_factor.shape, F32),
            jax.ShapeDtypeStruct(right_factor.shape, F32),
        ),
        in_specs=[vmem_spec] * 3,
        out_specs=(any_spec,) * 4,
        scratch_shapes=[dma((2 + 2 * NB,))],
        compiler_params=pltpu.CompilerParams(vmem_limit_bytes=1 << 20),
        name="write",
    )(*held)


def solution(mesh):
    in_specs = (P("dp", "feat"), P("feat", None, None), P("feat", None, None), P("dp", "feat"))
    out_specs = (P("dp", "feat"), P("dp", "feat"), P("feat", None, None), P("feat", None, None))
    return jax.shard_map(local, mesh=mesh, in_specs=in_specs, out_specs=out_specs, check_vma=False)
```
